32 devices in a mesh: iblk: 4 (over x, core), jblk: 8 (over z, y).
Axes of the slice: x: 2, y: 2, z: 4, core: 2. Of those that a mesh axis runs over, the one named last changes fastest.
Arguments:
- pno_basis: bfloat16 [4, 8, 4, 512, 128], P('iblk', 'jblk'), may hold values from -0.5 to 0.5
- amplitudes: bfloat16 [4, 8, 4, 128, 128], P('iblk', 'jblk'), may hold values from -6 to 6
- pno_energy: float32 [4, 8, 4, 128], P('iblk', 'jblk'), may hold values from 0.5 to 2
- fock_values: float32 [256], replicated, may hold values from -0.4 to 0.4
- couplings: int32 [4, 8, 4, 3, 12], P('iblk', 'jblk'), may hold values from 0 to 255, as said below
- counts: int32 [4, 8, 4], P('iblk', 'jblk'), may hold values from 3 to 12, as said below
Outputs:
- residual: float32 [4, 8, 4, 128, 128], P('iblk', 'jblk')
The draws below stay inside these ranges and needn't reach their ends.
Inputs may be any that keep to these rules, and one draw needn't show every extreme that they name: `couplings`: rows 0 and 1 hold pair numbers below 4, row 2 holds Fock table entries below 256; within one block of pairs and block step, each combination of local pair and visiting pair stands in at most one slot, live or not; slots at or after the live count are unused. `counts`: some block of pairs fills all 12 slots in some block step in every draw.
All inputs are finite; a program needn't handle non-finite values.
Results may differ from the reference program's by a relative error of at most 0.003.
Values may be sent and summed in bfloat16 or wider, within the bound.
No kernel may reach another device: no remote copies, remote signals or barrier semaphores. Data moves between devices by JAX's collectives and lax.ppermute only.
A program may use at most 64 MiB of HBM per device.

```python
import math
import jax
import jax.numpy as jnp
from jax import lax

NPAO = 512
NPNO = 128
PAIRS_DEV = 4
SLOTS = 12
REACH = 2
STEPS = 4
FOCK = 256
IBLOCKS = 4
JBLOCKS = 8


def draw_couplings(key, part):
    array_shape = (IBLOCKS, JBLOCKS, STEPS, 1, SLOTS)
    keys = jax.random.split(jax.random.fold_in(key, 23), 2)
    combo_keys = jax.random.split(keys[0], IBLOCKS * JBLOCKS * STEPS)
    combos = jax.vmap(lambda one_key: jax.random.permutation(one_key, PAIRS_DEV * PAIRS_DEV)[:SLOTS])(combo_keys)
    combos = combos.astype(jnp.int32).reshape(array_shape)
    local_pairs = combos // PAIRS_DEV
    visit_pairs = combos % PAIRS_DEV
    fock_entries = jax.random.randint(keys[1], array_shape, 0, FOCK, dtype=jnp.int32)
    fock_entries = fock_entries.at[0, 0, 0, 0, 0].set(FOCK - 1)
    return jnp.concatenate([local_pairs, visit_pairs, fock_entries], axis=3)


def draw_counts(key, part):
    array_shape = (IBLOCKS, JBLOCKS, STEPS)
    keys = jax.random.split(jax.random.fold_in(key, 11), 2)
    drawn = jax.random.randint(keys[0], array_shape, max(SLOTS // 4, 1), SLOTS + 1, dtype=jnp.int32)
    flattened = drawn.reshape(-1)
    chosen_slot = jax.random.randint(keys[1], (), 0, flattened.shape[0], dtype=jnp.int32)
    flattened = flattened.at[chosen_slot].set(SLOTS)
    return flattened.reshape(array_shape)


def block_scale(own_key, shape, cuts, smallest, top_value):
    loudness = 1.0
    for dim, blocks in cuts:
        draws = jax.random.uniform(jax.random.fold_in(jax.random.fold_in(own_key, 6), dim), (blocks,), jnp.float32, smallest / len(cuts), top_value / len(cuts))
        loudness = loudness * jnp.repeat(jnp.exp(draws), shape[dim] // blocks).reshape((-1,) + (1,) * (len(shape) - 1 - dim))
    return loudness


def gaussian(rng, shape, spread, limit, cuts=(), kind=jnp.bfloat16):
    result = jax.random.normal(rng, shape, jnp.float32) * spread
    if len(cuts) > 0:
        result = block_scale(rng, shape, cuts, -0.22, 0.18) * result
    return jnp.clip(result, min=-limit, max=limit).astype(kind)


def setup_inputs(seed: int = 0) -> dict:
    streams_of = jax.random.split(jax.random.key(seed), 7)
    return {
        "pno_basis": gaussian(streams_of[0], (IBLOCKS, JBLOCKS, PAIRS_DEV, NPAO, NPNO), 0.0625, 0.5, ((0, 4), (1, 8))),
        "amplitudes": gaussian(streams_of[1], (IBLOCKS, JBLOCKS, PAIRS_DEV, NPNO, NPNO), 1.0, 6.0, ((0, 4), (1, 8))),
        "pno_energy": jnp.clip(jnp.exp(math.log(2.0) - 1.3862944 * jax.random.uniform(streams_of[2], (IBLOCKS, JBLOCKS, PAIRS_DEV, NPNO), jnp.float32) ** block_scale(streams_of[2], (IBLOCKS, JBLOCKS, PAIRS_DEV, NPNO), ((0, 4), (1, 8)), -0.2, 0.2)), 0.5, 2.0),
        "fock_values": jnp.clip(jax.random.uniform(streams_of[3], (FOCK,), jnp.float32, -0.4, 0.4), -0.4, 0.4),
        "couplings": draw_couplings(jax.random.fold_in(streams_of[6], 71), 0),
        "counts": draw_counts(jax.random.fold_in(streams_of[6], 71), 0),
    }


def lookup_weights(fock_index, live_count, fock_values):
    table_ids = lax.iota(jnp.int32, fock_values.shape[0])
    slot_ids = lax.iota(jnp.int32, fock_index.shape[0])
    picked = jnp.sum(jnp.where(fock_index[:, None] == table_ids[None, :], fock_values[None, :], jnp.float32(0.0)), axis=1)
    return jnp.where(slot_ids < live_count, picked, jnp.float32(0.0))


def rounded(value):
    return lax.optimization_barrier(value.astype(jnp.bfloat16)).astype(jnp.float32)


def coupling_terms(couple_plan, live_count, own_basis, own_amps, visit_basis, visit_amps, fock_values):
    highest = lax.Precision.HIGHEST
    local_index = couple_plan[0]
    visit_index = couple_plan[1]
    weight = lookup_weights(couple_plan[2], live_count, fock_values)
    intersection = jnp.einsum("cmp,cmq->cpq", own_basis[local_index].astype(jnp.float32), visit_basis[visit_index].astype(jnp.float32), precision=highest)
    intersection = rounded(intersection)
    left_half = rounded(jnp.einsum("cpq,cqr->cpr", intersection, visit_amps[visit_index].astype(jnp.float32), precision=highest))
    local_terms = jnp.einsum("cpr,csr->cps", left_half, intersection, precision=highest)
    right_half = rounded(jnp.einsum("cpq,cpr->cqr", intersection, own_amps[local_index].astype(jnp.float32), precision=highest))
    visit_terms = jnp.einsum("cqr,crs->cqs", right_half, intersection, precision=highest)
    pair_ids = lax.iota(jnp.int32, own_basis.shape[0])
    to_local = jnp.where(local_index[None, :] == pair_ids[:, None], weight[None, :], jnp.float32(0.0))
    to_visit = jnp.where(visit_index[None, :] == pair_ids[:, None], weight[None, :], jnp.float32(0.0))
    width = intersection.shape[1]
    slot_total = local_index.shape[0]
    local_add = jnp.dot(to_local, local_terms.reshape(slot_total, -1), precision=highest).reshape(pair_ids.shape[0], width, width)
    visit_add = jnp.dot(to_visit, visit_terms.reshape(slot_total, -1), precision=highest).reshape(pair_ids.shape[0], width, width)
    return local_add, visit_add


def reference(pno_basis, amplitudes, pno_energy, fock_values, couplings, counts):
    def per_device(device_index):
        iblock = device_index // JBLOCKS
        jblock = device_index % JBLOCKS
        own_basis = pno_basis[iblock, jblock]
        own_amps = amplitudes[iblock, jblock]
        local_total = jnp.zeros(own_amps.shape, jnp.float32)
        visit_parts = []
        for block_step in range(STEPS):
            distance = block_step % REACH + 1
            if block_step < REACH:
                source_i = (iblock - distance) % IBLOCKS
                source_j = jblock
            else:
                source_i = iblock
                source_j = (jblock - distance) % JBLOCKS
            local_add, visit_add = coupling_terms(couplings[iblock, jblock, block_step], counts[iblock, jblock, block_step], own_basis, own_amps, pno_basis[source_i, source_j], amplitudes[source_i, source_j], fock_values)
            local_total = local_total + local_add
            visit_parts.append(visit_add)
        return local_total, jnp.stack(visit_parts)

    local_all, visit_all = lax.map(per_device, jnp.arange(IBLOCKS * JBLOCKS, dtype=jnp.int32))
    visit_all = visit_all.reshape((IBLOCKS, JBLOCKS, STEPS) + amplitudes.shape[2:])
    diagonal = pno_energy[..., :, None] + pno_energy[..., None, :]
    residual = diagonal * amplitudes.astype(jnp.float32) + local_all.reshape(amplitudes.shape)
    for block_step in range(STEPS):
        distance = block_step % REACH + 1
        axis_number = 0 if block_step < REACH else 1
        residual = residual + jnp.roll(visit_all[:, :, block_step], -distance, axis=axis_number)
    return residual
```

```python
import functools

import jax
import jax.numpy as jnp
from jax import lax
from jax.experimental import pallas as pl
from jax.experimental.pallas import tpu as pltpu
from jax.sharding import PartitionSpec as P

F32, BF16, I32 = jnp.float32, jnp.bfloat16, jnp.int32
AXES = ("iblk", "jblk")
PARTS = 3
ROLES = 4
OWN, PARTNER, HEAVY, LIGHT = range(ROLES)
OP, OH, PH, OL = range(4)
META = 16
LANES = 128


def routes(ni, nj):
    def flow(i, j):
        return (1 if j % 2 == 0 else -1), (1 if i % 2 == 1 else -1)

    def along_i(i, j):
        return (i - 2 * flow(i, j)[0]) % ni, j

    def along_j(i, j):
        return i, (j - 2 * flow(i, j)[1]) % nj

    def odd(i, j):
        return (i + j) % 2 == 1

    picks = (
        lambda i, j: (i ^ 1, j) if odd(i, j) else (i, j ^ 1),
        lambda i, j: along_i(i, j) if odd(i, j) else along_j(i, j),
        lambda i, j: along_j(i, j) if odd(i, j) else along_i(i, j),
    )
    made = []
    for pick in picks:
        pairs = []
        for i in range(ni):
            for j in range(nj):
                si, sj = pick(i, j)
                pairs.append((si * nj + sj, i * nj + j))
        made.append(pairs)
    return made


def moved(block, route):
    return lax.ppermute(block, AXES, route)


def back(route):
    return [(b, a) for a, b in route]


def dot(a, b):
    return lax.dot_general(a, b, (((1,), (0,)), ((), ())), preferred_element_type=F32)


def dot_nt(a, b):
    return lax.dot_general(a, b, (((1,), (1,)), ((), ())), preferred_element_type=F32)


def two_blocks(a, b):
    zero = jnp.zeros_like(a)
    return jnp.concatenate(
        [jnp.concatenate([a, zero], 1), jnp.concatenate([zero, b], 1)], 0
    )


def prep_kernel(reach, plan, counts, fock, basis, amps, sent, turned):
    pairs, _, width = amps.shape
    steps, _, slots = plan.shape
    i, j = lax.axis_index(AXES[0]) % 2, lax.axis_index(AXES[1]) % 2
    forward = (1 - j, i)
    i_heavy = (i + j) % 2
    lane = lax.broadcasted_iota(I32, (META, LANES), 1)
    row = lax.broadcasted_iota(I32, (META, LANES), 0)
    table = jnp.zeros((META, LANES), F32)
    for t in range(steps):
        axis, far = t // reach, t % reach
        heavy = i_heavy if axis == 0 else 1 - i_heavy
        ahead = forward[axis]
        if far:
            role_h, slot_h = jnp.where(ahead == 1, OWN, HEAVY), OH
            role_l, slot_l = jnp.where(ahead == 1, OWN, LIGHT), OL
        else:
            role_h, slot_h = jnp.where(ahead == 1, OWN, HEAVY), jnp.where(ahead == 1, OP, PH)
            role_l, slot_l = PARTNER, jnp.where(ahead == 1, PH, OP)
        role = jnp.where(heavy == 1, role_h, role_l)
        slot = jnp.where(heavy == 1, slot_h, slot_l)
        base = slot * (pairs * pairs)
        live = counts[t]

        def place(c, weight):
            p, q = plan[t, 0, c], plan[t, 1, c]
            at = base + jnp.where(ahead == 1, p * pairs + q, q * pairs + p)
            value = jnp.where(c < live, fock[plan[t, 2, c]], jnp.float32(0.0))
            return jnp.where(lane == at, value, weight)

        weight = lax.fori_loop(0, slots, place, jnp.zeros((META, LANES), F32), unroll=True)
        high = weight.astype(BF16).astype(F32)
        rest = weight - high
        middle = rest.astype(BF16).astype(F32)
        for part, piece in enumerate((high, middle, rest - middle)):
            table = jnp.where(row == part * ROLES + role, piece + table, table)
    sent[pl.ds(0, pairs * width), :] = amps[...].reshape(pairs * width, width)
    sent[pl.ds(pairs * width, META), :] = table.astype(BF16)
    for p in range(pairs):
        turned[pl.ds(p * width, width), :] = basis[p].T


def weight_rows(blocks, slot, pairs):
    row = jnp.zeros((1, LANES), F32)
    tables = [(table.astype(F32), role) for table, role in blocks]
    for part in range(PARTS):
        for table, role in tables:
            at = part * ROLES + role
            row = row + table[at : at + 1]
    shape = (pairs * pairs, LANES)
    mine = lax.broadcasted_iota(I32, shape, 1) == (
        slot * pairs * pairs + lax.broadcasted_iota(I32, shape, 0)
    )
    picked = jnp.sum(jnp.where(mine, row, jnp.float32(0.0)), axis=1, keepdims=True)
    wide = jnp.broadcast_to(picked, shape)
    return [[wide[p * pairs + q : p * pairs + q + 1] for q in range(pairs)] for p in range(pairs)]


def couple(turned, amps, other_basis, other_amps, weight, width):
    rows, columns = len(amps), len(other_amps)
    cut = lambda a, r, c: a[r * width : (r + 1) * width, c * width : (c + 1) * width]
    near = jnp.concatenate(
        [
            dot(turned, jnp.concatenate(other_basis[k : k + 2], 1)).astype(BF16)
            for k in range(0, columns, 2)
        ],
        1,
    )
    near_t = near.T
    left = jnp.concatenate(
        [
            dot(
                near[:, k * width : (k + 2) * width], two_blocks(other_amps[k], other_amps[k + 1])
            ).astype(BF16)
            for k in range(0, columns, 2)
        ],
        1,
    )
    right = jnp.concatenate(
        [
            dot(near_t[:, k * width : (k + 2) * width], two_blocks(amps[k], amps[k + 1])).astype(
                BF16
            )
            for k in range(0, rows, 2)
        ],
        1,
    )
    own, other = [], []
    for p in range(rows):
        own.append(
            sum(
                dot_nt(cut(left, p, q), cut(near, p, q)) * weight[p][q] for q in range(columns)
            )
        )
    for q in range(columns):
        other.append(
            sum(dot(cut(right, q, p), cut(near, p, q)) * weight[p][q] for p in range(rows))
        )
    return own, other


def amps_of(ref, pairs, width):
    return [ref[pl.ds(p * width, width), :] for p in range(pairs)]


def heavy_kernel(
    turned, own_sent, p_basis, p_sent, h_basis, h_sent, energy, total, p_back, h_back
):
    pairs, depth, width = p_basis.shape
    own_a, p_a, h_a = (amps_of(r, pairs, width) for r in (own_sent, p_sent, h_sent))
    meta = pl.ds(pairs * width, META)
    tables = ((own_sent[meta, :], OWN), (p_sent[meta, :], PARTNER), (h_sent[meta, :], HEAVY))
    p_b = [p_basis[p] for p in range(pairs)]
    h_b = [h_basis[p] for p in range(pairs)]
    own_t = turned[...]
    x1, y1 = couple(own_t, own_a, p_b, p_a, weight_rows(tables, OP, pairs), width)
    x2, y2 = couple(own_t, own_a, h_b, h_a, weight_rows(tables, OH, pairs), width)
    p_t = jnp.concatenate([b.T for b in p_b], 0)
    x3, y3 = couple(p_t, p_a, h_b, h_a, weight_rows(tables, PH, pairs), width)
    for p in range(pairs):
        across = jnp.broadcast_to(energy[pl.ds(p, 1), :], (width, width))
        diagonal = (across.T + across) * own_a[p].astype(F32)
        total[p] = diagonal + (x1[p] + x2[p])
        p_back[p] = (y1[p] + x3[p]).astype(BF16)
        h_back[p] = (y2[p] + y3[p]).astype(BF16)


def light_kernel(turned, own_sent, l_basis, l_sent, total_in, total, l_back):
    pairs, depth, width = l_basis.shape
    own_a, l_a = (amps_of(r, pairs, width) for r in (own_sent, l_sent))
    meta = pl.ds(pairs * width, META)
    tables = ((own_sent[meta, :], OWN), (l_sent[meta, :], LIGHT))
    l_b = [l_basis[p] for p in range(pairs)]
    x, y = couple(turned[...], own_a, l_b, l_a, weight_rows(tables, OL, pairs), width)
    for p in range(pairs):
        total[p] = total_in[p] + x[p]
        l_back[p] = y[p].astype(BF16)


def on_device(all_routes, reach, pno_basis, amplitudes, pno_energy, fock_values, couplings, counts):
    to_p, to_h, to_l = all_routes
    basis, amps, energy = pno_basis[0, 0], amplitudes[0, 0], pno_energy[0, 0]
    pairs, depth, width = basis.shape
    vmem, smem = pl.BlockSpec(memory_space=pltpu.VMEM), pl.BlockSpec(memory_space=pltpu.SMEM)
    params = pltpu.CompilerParams(vmem_limit_bytes=48 * 1024 * 1024)
    square = (pairs, width, width)
    sent, turned = pl.pallas_call(
        functools.partial(prep_kernel, reach),
        out_shape=(
            jax.ShapeDtypeStruct((pairs * width + META, width), BF16),
            jax.ShapeDtypeStruct((pairs * width, depth), BF16),
        ),
        in_specs=[smem, smem, smem, vmem, vmem],
        out_specs=(vmem, vmem),
        compiler_params=params,
        name="prep",
    )(couplings[0, 0], counts[0, 0], fock_values, basis, amps)
    h_basis, p_basis = moved(basis, to_h), moved(basis, to_p)
    h_sent, p_sent = moved(sent, to_h), moved(sent, to_p)
    l_basis, l_sent = moved(basis, to_l), moved(sent, to_l)
    flops = 2 * pairs * pairs * (width * width * depth + 4 * width**3)
    total, p_back, h_back = pl.pallas_call(
        heavy_kernel,
        out_shape=(
            jax.ShapeDtypeStruct(square, F32),
            jax.ShapeDtypeStruct(square, BF16),
            jax.ShapeDtypeStruct(square, BF16),
        ),
        in_specs=[vmem] * 7,
        out_specs=(vmem,) * 3,
        compiler_params=params,
        cost_estimate=pl.CostEstimate(
            flops=3 * flops, bytes_accessed=3 * basis.size * 2, transcendentals=0
        ),
        name="heavy",
    )(turned, sent, p_basis, p_sent, h_basis, h_sent, energy)
    total, l_back = pl.pallas_call(
        light_kernel,
        out_shape=(jax.ShapeDtypeStruct(square, F32), jax.ShapeDtypeStruct(square, BF16)),
        in_specs=[vmem] * 5,
        out_specs=(vmem,) * 2,
        compiler_params=params,
        cost_estimate=pl.CostEstimate(
            flops=flops, bytes_accessed=basis.size * 2, transcendentals=0
        ),
        name="light",
    )(turned, sent, l_basis, l_sent, total)
    for piece, route in ((p_back, to_p), (h_back, to_h), (l_back, to_l)):
        total = total + moved(piece, back(route)).astype(F32)
    return total[None, None]


def solution(mesh):
    ni, nj = (mesh.shape[a] for a in AXES)
    assert ni % 2 == 0 and nj % 2 == 0 and min(ni, nj) > 2
    placed = (
        P("iblk", "jblk", None, None, None),
        P("iblk", "jblk", None, None, None),
        P("iblk", "jblk", None, None),
        P(),
        P("iblk", "jblk", None, None, None),
        P("iblk", "jblk", None),
    )
    return jax.shard_map(
        functools.partial(on_device, routes(ni, nj), 2),
        mesh=mesh,
        in_specs=placed,
        out_specs=P("iblk", "jblk", None, None, None),
        check_vma=False,
    )
```

```python
import functools

import jax
import jax.numpy as jnp
from jax import lax
from jax.experimental import pallas as pl
from jax.experimental.pallas import tpu as pltpu
from jax.sharding import PartitionSpec as P


F32, BF16, I32 = jnp.float32, jnp.bfloat16, jnp.int32
AXES = ("iblk", "jblk")
PARTS = 3
ROLES = 4
OWN, PARTNER, HEAVY, LIGHT = range(ROLES)
OP, OH, PH, OL = range(4)
META = 16
LANES = 128


def routes(ni, nj):
    def flow(i, j):
        return (1 if j % 2 == 0 else -1), (1 if i % 2 == 1 else -1)

    def along_i(i, j):
        return (i - 2 * flow(i, j)[0]) % ni, j

    def along_j(i, j):
        return i, (j - 2 * flow(i, j)[1]) % nj

    def odd(i, j):
        return (i + j) % 2 == 1

    picks = (
        lambda i, j: (i ^ 1, j) if odd(i, j) else (i, j ^ 1),
        lambda i, j: along_i(i, j) if odd(i, j) else along_j(i, j),
        lambda i, j: along_j(i, j) if odd(i, j) else along_i(i, j),
    )
    made = []
    for pick in picks:
        pairs = []
        for i in range(ni):
            for j in range(nj):
                si, sj = pick(i, j)
                pairs.append((si * nj + sj, i * nj + j))
        made.append(pairs)
    return made


def back(route):
    return [(b, a) for a, b in route]


def dot(a, b):
    return lax.dot_general(a, b, (((1,), (0,)), ((), ())), preferred_element_type=F32)


def dot_nt(a, b):
    return lax.dot_general(a, b, (((1,), (1,)), ((), ())), preferred_element_type=F32)


def two_blocks(a, b):
    zero = jnp.zeros_like(a)
    return jnp.concatenate(
        [jnp.concatenate([a, zero], 1), jnp.concatenate([zero, b], 1)], 0
    )


def prep_kernel(reach, plan_hbm, counts_hbm, fock_hbm, amps_hbm, sent, plan, counts, fock, sems):
    pairs, width, _ = amps_hbm.shape
    copies = [
        pltpu.make_async_copy(src, dst, sems.at[k])
        for k, (src, dst) in enumerate(
            [(plan_hbm, plan), (counts_hbm, counts), (fock_hbm, fock)]
            + [(amps_hbm.at[p], sent.at[pl.ds(p * width, width)]) for p in range(pairs)]
        )
    ]
    for copy in copies:
        copy.start()
    _, steps, slots = plan.shape
    i, j = lax.axis_index(AXES[0]) % 2, lax.axis_index(AXES[1]) % 2
    forward = (1 - j, i)
    i_heavy = (i + j) % 2
    lane = lax.broadcasted_iota(I32, (META, LANES), 1)
    row = lax.broadcasted_iota(I32, (META, LANES), 0)
    table = jnp.zeros((META, LANES), F32)
    for copy in copies[:3]:
        copy.wait()
    for t in range(steps):
        axis, far = t // reach, t % reach
        heavy = i_heavy if axis == 0 else 1 - i_heavy
        ahead = forward[axis]
        if far:
            role_h, slot_h = jnp.where(ahead == 1, OWN, HEAVY), OH
            role_l, slot_l = jnp.where(ahead == 1, OWN, LIGHT), OL
        else:
            role_h, slot_h = jnp.where(ahead == 1, OWN, HEAVY), jnp.where(ahead == 1, OP, PH)
            role_l, slot_l = PARTNER, jnp.where(ahead == 1, PH, OP)
        role = jnp.where(heavy == 1, role_h, role_l)
        slot = jnp.where(heavy == 1, slot_h, slot_l)
        base = slot * (pairs * pairs)
        live = counts[t]

        def place(c, weight):
            p, q = plan[0, t, c], plan[1, t, c]
            at = base + jnp.where(ahead == 1, p * pairs + q, q * pairs + p)
            value = jnp.where(c < live, fock[plan[2, t, c]], jnp.float32(0.0))
            return jnp.where(lane == at, value, weight)

        weight = lax.fori_loop(0, slots, place, jnp.zeros((META, LANES), F32), unroll=True)
        high = weight.astype(BF16).astype(F32)
        rest = weight - high
        middle = rest.astype(BF16).astype(F32)
        for part, piece in enumerate((high, middle, rest - middle)):
            table = jnp.where(row == part * ROLES + role, piece + table, table)
    sent[pl.ds(pairs * width, META), :] = table.astype(BF16)
    for copy in copies[3:]:
        copy.wait()


def weight_rows(blocks, slot, pairs):
    row = jnp.zeros((1, LANES), F32)
    tables = [(table.astype(F32), role) for table, role in blocks]
    for part in range(PARTS):
        for table, role in tables:
            at = part * ROLES + role
            row = row + table[at : at + 1]
    shape = (pairs * pairs, LANES)
    mine = lax.broadcasted_iota(I32, shape, 1) == (
        slot * pairs * pairs + lax.broadcasted_iota(I32, shape, 0)
    )
    picked = jnp.sum(jnp.where(mine, row, jnp.float32(0.0)), axis=1, keepdims=True)
    wide = jnp.broadcast_to(picked, shape)
    return [[wide[p * pairs + q : p * pairs + q + 1] for q in range(pairs)] for p in range(pairs)]


def couple(turned, amps, other_basis, other_amps, weight, width):
    rows, columns = len(amps), len(other_amps)
    cut = lambda a, r, c: a[r * width : (r + 1) * width, c * width : (c + 1) * width]
    near = jnp.concatenate(
        [
            dot(turned, jnp.concatenate(other_basis[k : k + 2], 1)).astype(BF16)
            for k in range(0, columns, 2)
        ],
        1,
    )
    near_t = near.T
    left = jnp.concatenate(
        [
            dot(
                near[:, k * width : (k + 2) * width], two_blocks(other_amps[k], other_amps[k + 1])
            ).astype(BF16)
            for k in range(0, columns, 2)
        ],
        1,
    )
    right = jnp.concatenate(
        [
            dot(near_t[:, k * width : (k + 2) * width], two_blocks(amps[k], amps[k + 1])).astype(
                BF16
            )
            for k in range(0, rows, 2)
        ],
        1,
    )
    own, other = [], []
    for p in range(rows):
        own.append(
            sum(
                dot_nt(cut(left, p, q), cut(near, p, q)) * weight[p][q] for q in range(columns)
            )
        )
    for q in range(columns):
        other.append(
            sum(dot(cut(right, q, p), cut(near, p, q)) * weight[p][q] for p in range(rows))
        )
    return own, other


def amps_of(ref, pairs, width, first=0):
    return [ref[pl.ds(first + p * width, width), :] for p in range(pairs)]


def turn_kernel(basis, turned):
    pairs, _, width = basis.shape
    for p in range(pairs):
        turned[pl.ds(p * width, width), :] = basis[p].T


def near_kernel(own_turned, own_sent, p_basis, p_sent, energy, p_turned, total, p_sum):
    pairs, _, width = p_basis.shape
    own_a, p_a = (amps_of(r, pairs, width) for r in (own_sent, p_sent))
    meta = pl.ds(pairs * width, META)
    tables = ((own_sent[meta, :], OWN), (p_sent[meta, :], PARTNER))
    p_b = [p_basis[p] for p in range(pairs)]
    for p in range(pairs):
        p_turned[pl.ds(p * width, width), :] = p_b[p].T
    x, y = couple(own_turned[...], own_a, p_b, p_a, weight_rows(tables, OP, pairs), width)
    for p in range(pairs):
        across = jnp.broadcast_to(energy[pl.ds(p, 1), :], (width, width))
        total[p] = (across.T + across) * own_a[p].astype(F32) + x[p]
        p_sum[p] = y[p]


def heavy_kernel(
    own_turned, p_turned, own_sent, p_sent, h_basis, h_sent, total_in, p_sum,
    total, p_back, h_back,
):
    pairs, _, width = h_basis.shape
    own_a, p_a, h_a = (amps_of(r, pairs, width) for r in (own_sent, p_sent, h_sent))
    meta = pl.ds(pairs * width, META)
    tables = ((own_sent[meta, :], OWN), (p_sent[meta, :], PARTNER), (h_sent[meta, :], HEAVY))
    h_b = [h_basis[p] for p in range(pairs)]
    weight = weight_rows(tables, OH, pairs) + weight_rows(tables, PH, pairs)
    turned = jnp.concatenate([own_turned[...], p_turned[...]], 0)
    x, y = couple(turned, own_a + p_a, h_b, h_a, weight, width)
    for p in range(pairs):
        total[p] = total_in[p] + x[p]
        p_back[p] = (p_sum[p] + x[pairs + p]).astype(BF16)
        h_back[p] = y[p].astype(BF16)


def light_kernel(own_turned, own_sent, l_basis, l_sent, total_in, total, l_back):
    pairs, _, width = l_basis.shape
    own_a, l_a = (amps_of(r, pairs, width) for r in (own_sent, l_sent))
    meta = pl.ds(pairs * width, META)
    tables = ((own_sent[meta, :], OWN), (l_sent[meta, :], LIGHT))
    l_b = [l_basis[p] for p in range(pairs)]
    x, y = couple(own_turned[...], own_a, l_b, l_a, weight_rows(tables, OL, pairs), width)
    for p in range(pairs):
        total[p] = total_in[p] + x[p]
        l_back[p] = y[p].astype(BF16)


def on_device(all_routes, reach, pno_basis, amplitudes, pno_energy, fock_values, couplings, counts):
    to_p, to_h, to_l = all_routes
    basis, amps, energy = pno_basis[0, 0], amplitudes[0, 0], pno_energy[0, 0]
    plan, live = couplings[0, 0].transpose(1, 0, 2), counts[0, 0]
    pairs, depth, width = basis.shape
    vmem, hbm = pl.BlockSpec(memory_space=pltpu.VMEM), pl.BlockSpec(memory_space=pl.ANY)
    params = pltpu.CompilerParams(vmem_limit_bytes=48 * 1024 * 1024)
    square = (pairs, width, width)
    wide = jax.ShapeDtypeStruct(square, F32)
    narrow = jax.ShapeDtypeStruct(square, BF16)

    def moved(block, route):
        return lax.ppermute(block, AXES, route)

    def kernel(body, terms, shapes, *operands):
        flops = 2 * pairs * pairs * (width * width * depth + 4 * width**3)
        return pl.pallas_call(
            body,
            out_shape=shapes,
            in_specs=[vmem] * len(operands),
            out_specs=(vmem,) * len(shapes),
            compiler_params=params,
            cost_estimate=pl.CostEstimate(
                flops=terms * flops, bytes_accessed=2 * basis.size, transcendentals=0
            ),
        )(*operands)

    h_basis = moved(basis, to_h)
    p_basis = moved(basis, to_p)
    sent = pl.pallas_call(
        functools.partial(prep_kernel, reach),
        out_shape=jax.ShapeDtypeStruct((pairs * width + META, width), BF16),
        in_specs=[hbm] * 4,
        out_specs=vmem,
        scratch_shapes=[
            pltpu.SMEM(plan.shape, I32),
            pltpu.SMEM(live.shape, I32),
            pltpu.SMEM(fock_values.shape, F32),
            pltpu.SemaphoreType.DMA((3 + pairs,)),
        ],
        compiler_params=params,
        name="prep",
    )(*(pltpu.with_memory_space_constraint(x, pltpu.HBM) for x in (plan, live, fock_values, amps)))
    h_sent = moved(sent, to_h)
    p_sent = moved(sent, to_p)
    l_basis = moved(basis, to_l)
    l_sent = moved(sent, to_l)
    flat = jax.ShapeDtypeStruct((pairs * width, depth), BF16)
    (turned,) = kernel(turn_kernel, 0, (flat,), basis)
    p_turned, total, p_sum = kernel(
        near_kernel, 1, (flat, wide, wide), *(turned, sent, p_basis, p_sent, energy)
    )
    total, p_back, h_back = kernel(
        heavy_kernel,
        2,
        (wide, narrow, narrow),
        *(turned, p_turned, sent, p_sent, h_basis, h_sent, total, p_sum),
    )
    total, l_back = kernel(light_kernel, 1, (wide, narrow), turned, sent, l_basis, l_sent, total)
    for piece, route in ((h_back, to_h), (p_back, to_p), (l_back, to_l)):
        total = total + moved(piece, back(route)).astype(F32)
    return total[None, None]


def solution(mesh):
    ni, nj = (mesh.shape[a] for a in AXES)
    assert ni % 2 == 0 and nj % 2 == 0 and min(ni, nj) > 2
    placed = (
        P("iblk", "jblk", None, None, None),
        P("iblk", "jblk", None, None, None),
        P("iblk", "jblk", None, None),
        P(),
        P("iblk", "jblk", None, None, None),
        P("iblk", "jblk", None),
    )

    def body(*arguments):
        return on_device(routes(ni, nj), 2, *arguments)

    return jax.shard_map(
        body,
        mesh=mesh,
        in_specs=placed,
        out_specs=P("iblk", "jblk", None, None, None),
        check_vma=False,
    )
```

```python
import functools

import jax
import jax.numpy as jnp
from jax import lax
from jax.experimental import pallas as pl
from jax.experimental.pallas import tpu as pltpu
from jax.sharding import PartitionSpec as P


F32, BF16, I32 = jnp.float32, jnp.bfloat16, jnp.int32
AXES = ("iblk", "jblk")
PARTS = 3
ROLES = 4
OWN, PARTNER, HEAVY, LIGHT = range(ROLES)
OP, OH, PH, OL = range(4)
META = 16
LANES = 128


def routes(ni, nj):
    def flow(i, j):
        return (1 if j % 2 == 0 else -1), (1 if i % 2 == 1 else -1)

    def along_i(i, j):
        return (i - 2 * flow(i, j)[0]) % ni, j

    def along_j(i, j):
        return i, (j - 2 * flow(i, j)[1]) % nj

    def odd(i, j):
        return (i + j) % 2 == 1

    picks = (
        lambda i, j: (i ^ 1, j) if odd(i, j) else (i, j ^ 1),
        lambda i, j: along_i(i, j) if odd(i, j) else along_j(i, j),
        lambda i, j: along_j(i, j) if odd(i, j) else along_i(i, j),
    )
    made = []
    for pick in picks:
        pairs = []
        for i in range(ni):
            for j in range(nj):
                si, sj = pick(i, j)
                pairs.append((si * nj + sj, i * nj + j))
        made.append(pairs)
    return made


def back(route):
    return [(b, a) for a, b in route]


def dot(a, b):
    return lax.dot_general(a, b, (((1,), (0,)), ((), ())), preferred_element_type=F32)


def dot_nt(a, b):
    return lax.dot_general(a, b, (((1,), (1,)), ((), ())), preferred_element_type=F32)


def two_blocks(a, b):
    zero = jnp.zeros_like(a)
    return jnp.concatenate(
        [jnp.concatenate([a, zero], 1), jnp.concatenate([zero, b], 1)], 0
    )


def prep_kernel(reach, plan_hbm, counts_hbm, fock_hbm, amps_hbm, sent, plan, counts, fock, sems):
    pairs, width, _ = amps_hbm.shape
    copies = [
        pltpu.make_async_copy(src, dst, sems.at[k])
        for k, (src, dst) in enumerate(
            [(plan_hbm, plan), (counts_hbm, counts), (fock_hbm, fock)]
            + [(amps_hbm.at[p], sent.at[pl.ds(p * width, width)]) for p in range(pairs)]
        )
    ]
    for copy in copies:
        copy.start()
    _, steps, slots = plan.shape
    i, j = lax.axis_index(AXES[0]) % 2, lax.axis_index(AXES[1]) % 2
    forward = (1 - j, i)
    i_heavy = (i + j) % 2
    lane = lax.broadcasted_iota(I32, (META, LANES), 1)
    row = lax.broadcasted_iota(I32, (META, LANES), 0)
    table = jnp.zeros((META, LANES), F32)
    for copy in copies[:3]:
        copy.wait()
    for t in range(steps):
        axis, far = t // reach, t % reach
        heavy = i_heavy if axis == 0 else 1 - i_heavy
        ahead = forward[axis]
        if far:
            role_h, slot_h = jnp.where(ahead == 1, OWN, HEAVY), OH
            role_l, slot_l = jnp.where(ahead == 1, OWN, LIGHT), OL
        else:
            role_h, slot_h = jnp.where(ahead == 1, OWN, HEAVY), jnp.where(ahead == 1, OP, PH)
            role_l, slot_l = PARTNER, jnp.where(ahead == 1, PH, OP)
        role = jnp.where(heavy == 1, role_h, role_l)
        slot = jnp.where(heavy == 1, slot_h, slot_l)
        base = slot * (pairs * pairs)
        live = counts[t]

        def place(c, weight):
            p, q = plan[0, t, c], plan[1, t, c]
            at = base + jnp.where(ahead == 1, p * pairs + q, q * pairs + p)
            value = jnp.where(c < live, fock[plan[2, t, c]], jnp.float32(0.0))
            return jnp.where(lane == at, value, weight)

        weight = lax.fori_loop(0, slots, place, jnp.zeros((META, LANES), F32), unroll=True)
        high = weight.astype(BF16).astype(F32)
        rest = weight - high
        middle = rest.astype(BF16).astype(F32)
        for part, piece in enumerate((high, middle, rest - middle)):
            table = jnp.where(row == part * ROLES + role, piece + table, table)
    sent[pl.ds(pairs * width, META), :] = table.astype(BF16)
    for copy in copies[3:]:
        copy.wait()


def weight_rows(blocks, slot, pairs):
    row = jnp.zeros((1, LANES), F32)
    tables = [(table.astype(F32), role) for table, role in blocks]
    for part in range(PARTS):
        for table, role in tables:
            at = part * ROLES + role
            row = row + table[at : at + 1]
    shape = (pairs * pairs, LANES)
    mine = lax.broadcasted_iota(I32, shape, 1) == (
        slot * pairs * pairs + lax.broadcasted_iota(I32, shape, 0)
    )
    picked = jnp.sum(jnp.where(mine, row, jnp.float32(0.0)), axis=1, keepdims=True)
    wide = jnp.broadcast_to(picked, shape)
    return [[wide[p * pairs + q : p * pairs + q + 1] for q in range(pairs)] for p in range(pairs)]


def cut(a, r, c, width):
    return a[r * width : (r + 1) * width, c * width : (c + 1) * width]


def intersections(turned, basis):
    return jnp.concatenate(
        [
            dot(turned, jnp.concatenate(basis[k : k + 2], 1)).astype(BF16)
            for k in range(0, len(basis), 2)
        ],
        1,
    )


def half(near, amps, width):
    return jnp.concatenate(
        [
            dot(near[:, k * width : (k + 2) * width], two_blocks(amps[k], amps[k + 1])).astype(BF16)
            for k in range(0, len(amps), 2)
        ],
        1,
    )


def row_terms(near, column_amps, weight, width):
    left = half(near, column_amps, width)
    return [
        sum(
            dot_nt(cut(left, p, q, width), cut(near, p, q, width)) * weight[p][q]
            for q in range(len(column_amps))
        )
        for p in range(len(weight))
    ]


def column_sums(near, right, weight, width):
    return [
        sum(
            dot(cut(right, q, p, width), cut(near, p, q, width)) * weight[p][q]
            for p in range(len(weight))
        )
        for q in range(len(weight[0]))
    ]


def column_terms(near, row_amps, weight, width):
    return column_sums(near, half(near.T, row_amps, width), weight, width)


def bases_of(ref):
    return [ref[p] for p in range(ref.shape[0])]


def amps_of(ref, width):
    return [ref[pl.ds(p * width, width), :] for p in range((ref.shape[0] - META) // width)]


def table_of(ref, role):
    return ref[pl.ds(ref.shape[0] - META, META), :], role


def turn_kernel(basis, turned):
    pairs, _, width = basis.shape
    for p in range(pairs):
        turned[pl.ds(p * width, width), :] = basis[p].T


def near_kernel(own_turned, own_sent, p_basis, p_sent, energy, p_turned, total, p_sum):
    pairs, _, width = p_basis.shape
    bases, amps = bases_of(p_basis), amps_of(own_sent, width)
    for p in range(pairs):
        p_turned[pl.ds(p * width, width), :] = bases[p].T
    weight = weight_rows((table_of(own_sent, OWN), table_of(p_sent, PARTNER)), OP, pairs)
    near = intersections(own_turned[...], bases)
    x = row_terms(near, amps_of(p_sent, width), weight, width)
    y = column_terms(near, amps, weight, width)
    for p in range(pairs):
        across = jnp.broadcast_to(energy[pl.ds(p, 1), :], (width, width))
        total[p] = (across.T + across) * amps[p].astype(F32) + x[p]
        p_sum[p] = y[p]


def heavy_kernel(
    own_turned, p_turned, own_sent, p_sent, h_basis, h_sent, total_in, p_sum,
    total, p_back, h_back,
):
    pairs, _, width = h_basis.shape
    tables = (table_of(own_sent, OWN), table_of(p_sent, PARTNER), table_of(h_sent, HEAVY))
    weight = weight_rows(tables, OH, pairs) + weight_rows(tables, PH, pairs)
    turned = jnp.concatenate([own_turned[...], p_turned[...]], 0)
    near = intersections(turned, bases_of(h_basis))
    y = column_terms(near, amps_of(own_sent, width) + amps_of(p_sent, width), weight, width)
    x = row_terms(near, amps_of(h_sent, width), weight, width)
    for p in range(pairs):
        total[p] = total_in[p] + x[p]
        p_back[p] = (p_sum[p] + x[pairs + p]).astype(BF16)
        h_back[p] = y[p].astype(BF16)


def cross_kernel(own_turned, own_sent, l_basis, near, right):
    width = l_basis.shape[2]
    found = intersections(own_turned[...], bases_of(l_basis))
    near[...] = found
    right[...] = half(found.T, amps_of(own_sent, width), width)


def light_kernel(near, right, own_sent, l_sent, l_back):
    pairs, width, _ = l_back.shape
    weight = weight_rows((table_of(own_sent, OWN), table_of(l_sent, LIGHT)), OL, pairs)
    for p, y in enumerate(column_sums(near[...], right[...], weight, width)):
        l_back[p] = y.astype(BF16)


def rest_kernel(near, own_sent, l_sent, total_in, total):
    pairs, width, _ = total.shape
    weight = weight_rows((table_of(own_sent, OWN), table_of(l_sent, LIGHT)), OL, pairs)
    for p, x in enumerate(row_terms(near[...], amps_of(l_sent, width), weight, width)):
        total[p] = total_in[p] + x


def on_device(all_routes, reach, pno_basis, amplitudes, pno_energy, fock_values, couplings, counts):
    to_p, to_h, to_l = all_routes
    basis, amps, energy = pno_basis[0, 0], amplitudes[0, 0], pno_energy[0, 0]
    plan, live = couplings[0, 0].transpose(1, 0, 2), counts[0, 0]
    pairs, depth, width = basis.shape
    vmem, hbm = pl.BlockSpec(memory_space=pltpu.VMEM), pl.BlockSpec(memory_space=pl.ANY)
    params = pltpu.CompilerParams(vmem_limit_bytes=48 * 1024 * 1024)
    square = (pairs, width, width)
    wide = jax.ShapeDtypeStruct(square, F32)
    narrow = jax.ShapeDtypeStruct(square, BF16)
    flat = jax.ShapeDtypeStruct((pairs * width, depth), BF16)
    table = jax.ShapeDtypeStruct((pairs * width, pairs * width), BF16)

    def moved(block, route):
        return lax.ppermute(block, AXES, route)

    def kernel(body, terms, shapes, *operands):
        flops = 2 * pairs * pairs * (width * width * depth + 4 * width**3)
        return pl.pallas_call(
            body,
            out_shape=shapes,
            in_specs=[vmem] * len(operands),
            out_specs=(vmem,) * len(shapes),
            compiler_params=params,
            cost_estimate=pl.CostEstimate(
                flops=int(terms * flops), bytes_accessed=2 * basis.size, transcendentals=0
            ),
        )(*operands)

    h_basis = moved(basis, to_h)
    p_basis = moved(basis, to_p)
    given = (plan, live, fock_values, amps)
    sent = pl.pallas_call(
        functools.partial(prep_kernel, reach),
        out_shape=jax.ShapeDtypeStruct((pairs * width + META, width), BF16),
        in_specs=[hbm] * len(given),
        out_specs=vmem,
        scratch_shapes=[
            pltpu.SMEM(plan.shape, I32),
            pltpu.SMEM(live.shape, I32),
            pltpu.SMEM(fock_values.shape, F32),
            pltpu.SemaphoreType.DMA((3 + pairs,)),
        ],
        compiler_params=params,
        name="prep",
    )(*(pltpu.with_memory_space_constraint(x, pltpu.HBM) for x in given))
    h_sent, p_sent = moved(sent, to_h), moved(sent, to_p)
    l_basis, l_sent = moved(basis, to_l), moved(sent, to_l)
    (turned,) = kernel(turn_kernel, 0, (flat,), basis)
    p_turned, total, p_sum = kernel(
        near_kernel, 1, (flat, wide, wide), turned, sent, p_basis, p_sent, energy
    )
    total, p_back, h_back = kernel(
        heavy_kernel,
        2,
        (wide, narrow, narrow),
        *(turned, p_turned, sent, p_sent, h_basis, h_sent, total, p_sum),
    )
    near, right = kernel(cross_kernel, 0.5, (table, table), turned, sent, l_basis)
    (l_back,) = kernel(light_kernel, 0.2, (narrow,), near, right, sent, l_sent)
    (total,) = kernel(rest_kernel, 0.3, (wide,), near, sent, l_sent, total)
    for piece, route in ((h_back, to_h), (p_back, to_p), (l_back, to_l)):
        total = total + moved(piece, back(route)).astype(F32)
    return total[None, None]


def solution(mesh):
    ni, nj = (mesh.shape[a] for a in AXES)
    assert ni % 2 == 0 and nj % 2 == 0 and min(ni, nj) > 2
    placed = (
        P("iblk", "jblk", None, None, None),
        P("iblk", "jblk", None, None, None),
        P("iblk", "jblk", None, None),
        P(),
        P("iblk", "jblk", None, None, None),
        P("iblk", "jblk", None),
    )

    def body(*arguments):
        return on_device(routes(ni, nj), 2, *arguments)

    return jax.shard_map(
        body,
        mesh=mesh,
        in_specs=placed,
        out_specs=P("iblk", "jblk", None, None, None),
        check_vma=False,
    )
```

```python
import functools

import jax
import jax.numpy as jnp
from jax import lax
from jax.experimental import pallas as pl
from jax.experimental.pallas import tpu as pltpu
from jax.sharding import PartitionSpec as P


F32, BF16, I32 = jnp.float32, jnp.bfloat16, jnp.int32
AXES = ("iblk", "jblk")
PARTS = 3
ROLES = 4
OWN, PARTNER, HEAVY, LIGHT = range(ROLES)
OP, OH, PH, OL = range(4)
META = 16
LANES = 128


def routes(ni, nj):
    def flow(i, j):
        return (1 if j % 2 == 0 else -1), (1 if i % 2 == 1 else -1)

    def along_i(i, j):
        return (i - 2 * flow(i, j)[0]) % ni, j

    def along_j(i, j):
        return i, (j - 2 * flow(i, j)[1]) % nj

    def odd(i, j):
        return (i + j) % 2 == 1

    picks = (
        lambda i, j: (i ^ 1, j) if odd(i, j) else (i, j ^ 1),
        lambda i, j: along_i(i, j) if odd(i, j) else along_j(i, j),
        lambda i, j: along_j(i, j) if odd(i, j) else along_i(i, j),
    )
    made = []
    for pick in picks:
        pairs = []
        for i in range(ni):
            for j in range(nj):
                si, sj = pick(i, j)
                pairs.append((si * nj + sj, i * nj + j))
        made.append(pairs)
    return made


def back(route):
    return [(b, a) for a, b in route]


def dot(a, b):
    return lax.dot_general(a, b, (((1,), (0,)), ((), ())), preferred_element_type=F32)


def dot_nt(a, b):
    return lax.dot_general(a, b, (((1,), (1,)), ((), ())), preferred_element_type=F32)


def two_blocks(a, b):
    zero = jnp.zeros_like(a)
    return jnp.concatenate(
        [jnp.concatenate([a, zero], 1), jnp.concatenate([zero, b], 1)], 0
    )


def prep_kernel(
    reach, plan_hbm, counts_hbm, fock_hbm, amps_hbm, sent, table_out, plan, counts, fock, sems
):
    pairs, width, _ = amps_hbm.shape
    copies = [
        pltpu.make_async_copy(src, dst, sems.at[k])
        for k, (src, dst) in enumerate(
            [(plan_hbm, plan), (counts_hbm, counts), (fock_hbm, fock)]
            + [(amps_hbm.at[p], sent.at[pl.ds(p * width, width)]) for p in range(pairs)]
        )
    ]
    for copy in copies:
        copy.start()
    _, steps, slots = plan.shape
    i, j = lax.axis_index(AXES[0]) % 2, lax.axis_index(AXES[1]) % 2
    forward = (1 - j, i)
    i_heavy = (i + j) % 2
    lane = lax.broadcasted_iota(I32, (META, LANES), 1)
    row = lax.broadcasted_iota(I32, (META, LANES), 0)
    table = jnp.zeros((META, LANES), F32)
    for copy in copies[:3]:
        copy.wait()
    for t in range(steps):
        axis, far = t // reach, t % reach
        heavy = i_heavy if axis == 0 else 1 - i_heavy
        ahead = forward[axis]
        if far:
            role_h, slot_h = jnp.where(ahead == 1, OWN, HEAVY), OH
            role_l, slot_l = jnp.where(ahead == 1, OWN, LIGHT), OL
        else:
            role_h, slot_h = jnp.where(ahead == 1, OWN, HEAVY), jnp.where(ahead == 1, OP, PH)
            role_l, slot_l = PARTNER, jnp.where(ahead == 1, PH, OP)
        role = jnp.where(heavy == 1, role_h, role_l)
        slot = jnp.where(heavy == 1, slot_h, slot_l)
        base = slot * (pairs * pairs)
        live = counts[t]

        def place(c, weight):
            p, q = plan[0, t, c], plan[1, t, c]
            at = base + jnp.where(ahead == 1, p * pairs + q, q * pairs + p)
            value = jnp.where(c < live, fock[plan[2, t, c]], jnp.float32(0.0))
            return jnp.where(lane == at, value, weight)

        weight = lax.fori_loop(0, slots, place, jnp.zeros((META, LANES), F32), unroll=True)
        high = weight.astype(BF16).astype(F32)
        rest = weight - high
        middle = rest.astype(BF16).astype(F32)
        for part, piece in enumerate((high, middle, rest - middle)):
            table = jnp.where(row == part * ROLES + role, piece + table, table)
    sent[pl.ds(pairs * width, META), :] = table.astype(BF16)
    table_out[...] = table.astype(BF16)
    for copy in copies[3:]:
        copy.wait()


def weight_rows(blocks, slot, pairs):
    row = jnp.zeros((1, LANES), F32)
    tables = [(table.astype(F32), role) for table, role in blocks]
    for part in range(PARTS):
        for table, role in tables:
            at = part * ROLES + role
            row = row + table[at : at + 1]
    shape = (pairs * pairs, LANES)
    mine = lax.broadcasted_iota(I32, shape, 1) == (
        slot * pairs * pairs + lax.broadcasted_iota(I32, shape, 0)
    )
    picked = jnp.sum(jnp.where(mine, row, jnp.float32(0.0)), axis=1, keepdims=True)
    wide = jnp.broadcast_to(picked, shape)
    return [[wide[p * pairs + q : p * pairs + q + 1] for q in range(pairs)] for p in range(pairs)]


def cut(a, r, c, width):
    return a[r * width : (r + 1) * width, c * width : (c + 1) * width]


def intersections(turned, basis):
    return jnp.concatenate(
        [
            dot(turned, jnp.concatenate(basis[k : k + 2], 1)).astype(BF16)
            for k in range(0, len(basis), 2)
        ],
        1,
    )


def half(near, amps, width):
    return jnp.concatenate(
        [
            dot(near[:, k * width : (k + 2) * width], two_blocks(amps[k], amps[k + 1])).astype(BF16)
            for k in range(0, len(amps), 2)
        ],
        1,
    )


def row_terms(near, column_amps, weight, width):
    left = half(near, column_amps, width)
    return [
        sum(
            dot_nt(cut(left, p, q, width), cut(near, p, q, width)) * weight[p][q]
            for q in range(len(column_amps))
        )
        for p in range(len(weight))
    ]


def column_sums(near, right, weight, width):
    return [
        sum(
            dot(cut(right, q, p, width), cut(near, p, q, width)) * weight[p][q]
            for p in range(len(weight))
        )
        for q in range(len(weight[0]))
    ]


def column_terms(near, row_amps, weight, width):
    return column_sums(near, half(near.T, row_amps, width), weight, width)


def bases_of(ref):
    return [ref[p] for p in range(ref.shape[0])]


def amps_of(ref, width):
    return [ref[pl.ds(p * width, width), :] for p in range((ref.shape[0] - META) // width)]


def table_of(ref, role):
    return ref[pl.ds(ref.shape[0] - META, META), :], role


def turn_kernel(basis, turned):
    pairs, _, width = basis.shape
    for p in range(pairs):
        turned[pl.ds(p * width, width), :] = basis[p].T


def near_kernel(own_turned, own_sent, p_basis, p_sent, energy, p_turned, total, p_sum):
    pairs, _, width = p_basis.shape
    bases, amps = bases_of(p_basis), amps_of(own_sent, width)
    for p in range(pairs):
        p_turned[pl.ds(p * width, width), :] = bases[p].T
    weight = weight_rows((table_of(own_sent, OWN), table_of(p_sent, PARTNER)), OP, pairs)
    near = intersections(own_turned[...], bases)
    x = row_terms(near, amps_of(p_sent, width), weight, width)
    y = column_terms(near, amps, weight, width)
    for p in range(pairs):
        across = jnp.broadcast_to(energy[pl.ds(p, 1), :], (width, width))
        total[p] = (across.T + across) * amps[p].astype(F32) + x[p]
        p_sum[p] = y[p]


def heavy_kernel(
    own_turned, p_turned, own_sent, p_sent, h_basis, h_sent, total_in, p_sum,
    total, p_back, h_back,
):
    pairs, _, width = h_basis.shape
    tables = (table_of(own_sent, OWN), table_of(p_sent, PARTNER), table_of(h_sent, HEAVY))
    weight = weight_rows(tables, OH, pairs) + weight_rows(tables, PH, pairs)
    turned = jnp.concatenate([own_turned[...], p_turned[...]], 0)
    near = intersections(turned, bases_of(h_basis))
    y = column_terms(near, amps_of(own_sent, width) + amps_of(p_sent, width), weight, width)
    x = row_terms(near, amps_of(h_sent, width), weight, width)
    for p in range(pairs):
        total[p] = total_in[p] + x[p]
        p_back[p] = (p_sum[p] + x[pairs + p]).astype(BF16)
        h_back[p] = y[p].astype(BF16)


def cross_kernel(own_turned, own_sent, l_basis, near, right):
    width = l_basis.shape[2]
    found = intersections(own_turned[...], bases_of(l_basis))
    near[...] = found
    right[...] = half(found.T, amps_of(own_sent, width), width)


def light_kernel(near, right, own_table, l_table, l_back):
    pairs, width, _ = l_back.shape
    weight = weight_rows((table_of(own_table, OWN), table_of(l_table, LIGHT)), OL, pairs)
    for p, y in enumerate(column_sums(near[...], right[...], weight, width)):
        l_back[p] = y.astype(BF16)


def rest_kernel(near, own_sent, l_sent, total_in, total):
    pairs, width, _ = total.shape
    weight = weight_rows((table_of(own_sent, OWN), table_of(l_sent, LIGHT)), OL, pairs)
    for p, x in enumerate(row_terms(near[...], amps_of(l_sent, width), weight, width)):
        total[p] = total_in[p] + x


def on_device(all_routes, reach, pno_basis, amplitudes, pno_energy, fock_values, couplings, counts):
    to_p, to_h, to_l = all_routes
    basis, amps, energy = pno_basis[0, 0], amplitudes[0, 0], pno_energy[0, 0]
    plan, live = couplings[0, 0].transpose(1, 0, 2), counts[0, 0]
    pairs, depth, width = basis.shape
    vmem, hbm = pl.BlockSpec(memory_space=pltpu.VMEM), pl.BlockSpec(memory_space=pl.ANY)
    params = pltpu.CompilerParams(vmem_limit_bytes=48 * 1024 * 1024)
    square = (pairs, width, width)
    wide = jax.ShapeDtypeStruct(square, F32)
    narrow = jax.ShapeDtypeStruct(square, BF16)
    flat = jax.ShapeDtypeStruct((pairs * width, depth), BF16)
    table = jax.ShapeDtypeStruct((pairs * width, pairs * width), BF16)

    def moved(block, route):
        return lax.ppermute(block, AXES, route)

    def kernel(body, terms, shapes, *operands):
        flops = 2 * pairs * pairs * (width * width * depth + 4 * width**3)
        return pl.pallas_call(
            body,
            out_shape=shapes,
            in_specs=[vmem] * len(operands),
            out_specs=(vmem,) * len(shapes),
            compiler_params=params,
            cost_estimate=pl.CostEstimate(
                flops=int(terms * flops), bytes_accessed=2 * basis.size, transcendentals=0
            ),
        )(*operands)

    h_basis = moved(basis, to_h)
    p_basis = moved(basis, to_p)
    given = (plan, live, fock_values, amps)
    sent, rows = pl.pallas_call(
        functools.partial(prep_kernel, reach),
        out_shape=(
            jax.ShapeDtypeStruct((pairs * width + META, width), BF16),
            jax.ShapeDtypeStruct((META, LANES), BF16),
        ),
        in_specs=[hbm] * len(given),
        out_specs=(vmem, vmem),
        scratch_shapes=[
            pltpu.SMEM(plan.shape, I32),
            pltpu.SMEM(live.shape, I32),
            pltpu.SMEM(fock_values.shape, F32),
            pltpu.SemaphoreType.DMA((3 + pairs,)),
        ],
        compiler_params=params,
        name="prep",
    )(*(pltpu.with_memory_space_constraint(x, pltpu.HBM) for x in given))
    h_sent, p_sent = moved(sent, to_h), moved(sent, to_p)
    l_rows, l_basis, l_sent = (
        moved(what, to_l) for what in (rows, basis, sent)
    )
    (turned,) = kernel(turn_kernel, 0, (flat,), basis)
    p_turned, total, p_sum = kernel(
        near_kernel, 1, (flat, wide, wide), turned, sent, p_basis, p_sent, energy
    )
    total, p_back, h_back = kernel(
        heavy_kernel,
        2,
        (wide, narrow, narrow),
        *(turned, p_turned, sent, p_sent, h_basis, h_sent, total, p_sum),
    )
    near, right = kernel(cross_kernel, 0.5, (table, table), turned, sent, l_basis)
    (l_back,) = kernel(light_kernel, 0.2, (narrow,), near, right, rows, l_rows)
    (total,) = kernel(rest_kernel, 0.3, (wide,), near, sent, l_sent, total)
    for piece, route in ((h_back, to_h), (p_back, to_p), (l_back, to_l)):
        total = total + moved(piece, back(route)).astype(F32)
    return total[None, None]


def solution(mesh):
    ni, nj = (mesh.shape[a] for a in AXES)
    assert ni % 2 == 0 and nj % 2 == 0 and min(ni, nj) > 2
    placed = (
        P("iblk", "jblk", None, None, None),
        P("iblk", "jblk", None, None, None),
        P("iblk", "jblk", None, None),
        P(),
        P("iblk", "jblk", None, None, None),
        P("iblk", "jblk", None),
    )

    def body(*arguments):
        return on_device(routes(ni, nj), 2, *arguments)

    return jax.shard_map(
        body,
        mesh=mesh,
        in_specs=placed,
        out_specs=P("iblk", "jblk", None, None, None),
        check_vma=False,
    )
```

```python
import functools

import jax
import jax.numpy as jnp
from jax import lax
from jax.experimental import pallas as pl
from jax.experimental.pallas import tpu as pltpu
from jax.sharding import PartitionSpec as P


F32, BF16, I32 = jnp.float32, jnp.bfloat16, jnp.int32
AXES = ("iblk", "jblk")
PARTS = 3
ROLES = 4
OWN, PARTNER, HEAVY, LIGHT = range(ROLES)
OP, OH, PH, OL = range(4)
META = 16
LANES = 128


def routes(ni, nj):
    def flow(i, j):
        return (1 if j % 2 == 0 else -1), (1 if i % 2 == 1 else -1)

    def along_i(i, j):
        return (i - 2 * flow(i, j)[0]) % ni, j

    def along_j(i, j):
        return i, (j - 2 * flow(i, j)[1]) % nj

    def odd(i, j):
        return (i + j) % 2 == 1

    picks = (
        lambda i, j: (i ^ 1, j) if odd(i, j) else (i, j ^ 1),
        lambda i, j: along_i(i, j) if odd(i, j) else along_j(i, j),
        lambda i, j: along_j(i, j) if odd(i, j) else along_i(i, j),
    )
    made = []
    for pick in picks:
        pairs = []
        for i in range(ni):
            for j in range(nj):
                si, sj = pick(i, j)
                pairs.append((si * nj + sj, i * nj + j))
        made.append(pairs)
    return made


def back(route):
    return [(b, a) for a, b in route]


def dot(a, b):
    return lax.dot_general(a, b, (((1,), (0,)), ((), ())), preferred_element_type=F32)


def dot_nt(a, b):
    return lax.dot_general(a, b, (((1,), (1,)), ((), ())), preferred_element_type=F32)


def two_blocks(a, b):
    zero = jnp.zeros_like(a)
    return jnp.concatenate(
        [jnp.concatenate([a, zero], 1), jnp.concatenate([zero, b], 1)], 0
    )


def prep_kernel(
    reach, plan_hbm, counts_hbm, fock_hbm, amps_hbm, sent, table_out, plan, counts, fock, sems
):
    pairs, width, _ = amps_hbm.shape
    copies = [
        pltpu.make_async_copy(src, dst, sems.at[k])
        for k, (src, dst) in enumerate(
            [(plan_hbm, plan), (counts_hbm, counts), (fock_hbm, fock)]
            + [(amps_hbm.at[p], sent.at[pl.ds(p * width, width)]) for p in range(pairs)]
        )
    ]
    for copy in copies:
        copy.start()
    _, steps, slots = plan.shape
    i, j = lax.axis_index(AXES[0]) % 2, lax.axis_index(AXES[1]) % 2
    forward = (1 - j, i)
    i_heavy = (i + j) % 2
    lane = lax.broadcasted_iota(I32, (META, LANES), 1)
    row = lax.broadcasted_iota(I32, (META, LANES), 0)
    table = jnp.zeros((META, LANES), F32)
    for copy in copies[:3]:
        copy.wait()
    for t in range(steps):
        axis, far = t // reach, t % reach
        heavy = i_heavy if axis == 0 else 1 - i_heavy
        ahead = forward[axis]
        if far:
            role_h, slot_h = jnp.where(ahead == 1, OWN, HEAVY), OH
            role_l, slot_l = jnp.where(ahead == 1, OWN, LIGHT), OL
        else:
            role_h, slot_h = jnp.where(ahead == 1, OWN, HEAVY), jnp.where(ahead == 1, OP, PH)
            role_l, slot_l = PARTNER, jnp.where(ahead == 1, PH, OP)
        role = jnp.where(heavy == 1, role_h, role_l)
        slot = jnp.where(heavy == 1, slot_h, slot_l)
        base = slot * (pairs * pairs)
        live = counts[t]

        def place(c, weight):
            p, q = plan[0, t, c], plan[1, t, c]
            at = base + jnp.where(ahead == 1, p * pairs + q, q * pairs + p)
            value = jnp.where(c < live, fock[plan[2, t, c]], jnp.float32(0.0))
            return jnp.where(lane == at, value, weight)

        weight = lax.fori_loop(0, slots, place, jnp.zeros((META, LANES), F32), unroll=True)
        high = weight.astype(BF16).astype(F32)
        rest = weight - high
        middle = rest.astype(BF16).astype(F32)
        for part, piece in enumerate((high, middle, rest - middle)):
            table = jnp.where(row == part * ROLES + role, piece + table, table)
    sent[pl.ds(pairs * width, META), :] = table.astype(BF16)
    table_out[...] = table.astype(BF16)
    for copy in copies[3:]:
        copy.wait()


def weight_rows(blocks, slot, pairs):
    row = jnp.zeros((1, LANES), F32)
    tables = [(table.astype(F32), role) for table, role in blocks]
    for part in range(PARTS):
        for table, role in tables:
            at = part * ROLES + role
            row = row + table[at : at + 1]
    shape = (pairs * pairs, LANES)
    mine = lax.broadcasted_iota(I32, shape, 1) == (
        slot * pairs * pairs + lax.broadcasted_iota(I32, shape, 0)
    )
    picked = jnp.sum(jnp.where(mine, row, jnp.float32(0.0)), axis=1, keepdims=True)
    wide = jnp.broadcast_to(picked, shape)
    return [[wide[p * pairs + q : p * pairs + q + 1] for q in range(pairs)] for p in range(pairs)]


def cut(a, r, c, width):
    return a[r * width : (r + 1) * width, c * width : (c + 1) * width]


def intersections(turned, basis):
    return jnp.concatenate(
        [
            dot(turned, jnp.concatenate(basis[k : k + 2], 1)).astype(BF16)
            for k in range(0, len(basis), 2)
        ],
        1,
    )


def half(near, amps, width):
    return jnp.concatenate(
        [
            dot(near[:, k * width : (k + 2) * width], two_blocks(amps[k], amps[k + 1])).astype(BF16)
            for k in range(0, len(amps), 2)
        ],
        1,
    )


def row_terms(near, column_amps, weight, width):
    left = half(near, column_amps, width)
    return [
        sum(
            dot_nt(cut(left, p, q, width), cut(near, p, q, width)) * weight[p][q]
            for q in range(len(column_amps))
        )
        for p in range(len(weight))
    ]


def column_sums(near, right, weight, width):
    return [
        sum(
            dot(cut(right, q, p, width), cut(near, p, q, width)) * weight[p][q]
            for p in range(len(weight))
        )
        for q in range(len(weight[0]))
    ]


def column_terms(near, row_amps, weight, width):
    return column_sums(near, half(near.T, row_amps, width), weight, width)


def bases_of(ref):
    return [ref[p] for p in range(ref.shape[0])]


def amps_of(ref, width):
    return [ref[pl.ds(p * width, width), :] for p in range((ref.shape[0] - META) // width)]


def table_of(ref, role):
    return ref[pl.ds(ref.shape[0] - META, META), :], role


def turn_kernel(basis, turned):
    pairs, _, width = basis.shape
    for p in range(pairs):
        turned[pl.ds(p * width, width), :] = basis[p].T


def near_kernel(own_turned, own_sent, p_basis, p_sent, near, p_turned, p_sum):
    pairs, _, width = p_basis.shape
    bases = bases_of(p_basis)
    for p in range(pairs):
        p_turned[pl.ds(p * width, width), :] = bases[p].T
    weight = weight_rows((table_of(own_sent, OWN), table_of(p_sent, PARTNER)), OP, pairs)
    found = intersections(own_turned[...], bases)
    near[...] = found
    for p, y in enumerate(column_terms(found, amps_of(own_sent, width), weight, width)):
        p_sum[p] = y


def heavy_kernel(
    own_turned, p_turned, own_sent, p_sent, h_basis, h_sent, p_sum, near, p_back, h_back
):
    pairs, _, width = h_basis.shape
    tables = (table_of(own_sent, OWN), table_of(p_sent, PARTNER), table_of(h_sent, HEAVY))
    weight = weight_rows(tables, OH, pairs) + weight_rows(tables, PH, pairs)
    turned = jnp.concatenate([own_turned[...], p_turned[...]], 0)
    found = intersections(turned, bases_of(h_basis))
    near[...] = found[: pairs * width]
    y = column_terms(found, amps_of(own_sent, width) + amps_of(p_sent, width), weight, width)
    x = row_terms(found[pairs * width :], amps_of(h_sent, width), weight[pairs:], width)
    for p in range(pairs):
        p_back[p] = (p_sum[p] + x[p]).astype(BF16)
        h_back[p] = y[p].astype(BF16)


def cross_kernel(own_turned, own_sent, l_basis, near, right):
    width = l_basis.shape[2]
    found = intersections(own_turned[...], bases_of(l_basis))
    near[...] = found
    right[...] = half(found.T, amps_of(own_sent, width), width)


def light_kernel(near, right, own_table, l_table, l_back):
    pairs, width, _ = l_back.shape
    weight = weight_rows((table_of(own_table, OWN), table_of(l_table, LIGHT)), OL, pairs)
    for p, y in enumerate(column_sums(near[...], right[...], weight, width)):
        l_back[p] = y.astype(BF16)


def own_kernel(near_p, near_h, own_sent, p_sent, h_sent, energy, total):
    pairs, width, _ = total.shape
    tables = (table_of(own_sent, OWN), table_of(p_sent, PARTNER), table_of(h_sent, HEAVY))
    weight = weight_rows(tables, OP, pairs), weight_rows(tables, OH, pairs)
    x1 = row_terms(near_p[...], amps_of(p_sent, width), weight[0], width)
    x2 = row_terms(near_h[...], amps_of(h_sent, width), weight[1], width)
    for p, amps in enumerate(amps_of(own_sent, width)):
        across = jnp.broadcast_to(energy[pl.ds(p, 1), :], (width, width))
        total[p] = (across.T + across) * amps.astype(F32) + (x1[p] + x2[p])


def rest_kernel(near, own_sent, l_sent, total_in, total):
    pairs, width, _ = total.shape
    weight = weight_rows((table_of(own_sent, OWN), table_of(l_sent, LIGHT)), OL, pairs)
    for p, x in enumerate(row_terms(near[...], amps_of(l_sent, width), weight, width)):
        total[p] = total_in[p] + x


def on_device(all_routes, reach, pno_basis, amplitudes, pno_energy, fock_values, couplings, counts):
    to_p, to_h, to_l = all_routes
    basis, amps, energy = pno_basis[0, 0], amplitudes[0, 0], pno_energy[0, 0]
    plan, live = couplings[0, 0].transpose(1, 0, 2), counts[0, 0]
    pairs, depth, width = basis.shape
    vmem, hbm = pl.BlockSpec(memory_space=pltpu.VMEM), pl.BlockSpec(memory_space=pl.ANY)
    params = pltpu.CompilerParams(vmem_limit_bytes=48 * 1024 * 1024)
    square = (pairs, width, width)
    wide = jax.ShapeDtypeStruct(square, F32)
    narrow = jax.ShapeDtypeStruct(square, BF16)
    flat = jax.ShapeDtypeStruct((pairs * width, depth), BF16)
    table = jax.ShapeDtypeStruct((pairs * width, pairs * width), BF16)

    def moved(block, route):
        return lax.ppermute(block, AXES, route)

    def kernel(body, terms, shapes, *operands):
        flops = 2 * pairs * pairs * (width * width * depth + 4 * width**3)
        return pl.pallas_call(
            body,
            out_shape=shapes,
            in_specs=[vmem] * len(operands),
            out_specs=(vmem,) * len(shapes),
            compiler_params=params,
            cost_estimate=pl.CostEstimate(
                flops=int(terms * flops), bytes_accessed=2 * basis.size, transcendentals=0
            ),
        )(*operands)

    h_basis = moved(basis, to_h)
    p_basis = moved(basis, to_p)
    given = (plan, live, fock_values, amps)
    sent, rows = pl.pallas_call(
        functools.partial(prep_kernel, reach),
        out_shape=(
            jax.ShapeDtypeStruct((pairs * width + META, width), BF16),
            jax.ShapeDtypeStruct((META, LANES), BF16),
        ),
        in_specs=[hbm] * len(given),
        out_specs=(vmem, vmem),
        scratch_shapes=[
            pltpu.SMEM(plan.shape, I32),
            pltpu.SMEM(live.shape, I32),
            pltpu.SMEM(fock_values.shape, F32),
            pltpu.SemaphoreType.DMA((3 + pairs,)),
        ],
        compiler_params=params,
        name="prep",
    )(*(pltpu.with_memory_space_constraint(x, pltpu.HBM) for x in given))
    h_sent, p_sent = moved(sent, to_h), moved(sent, to_p)
    l_rows, l_basis, l_sent = (
        moved(what, to_l) for what in (rows, basis, sent)
    )
    (turned,) = kernel(turn_kernel, 0, (flat,), basis)
    near_p, p_turned, p_sum = kernel(
        near_kernel, 0.7, (table, flat, wide), turned, sent, p_basis, p_sent
    )
    near_h, p_back, h_back = kernel(
        heavy_kernel,
        1.7,
        (table, narrow, narrow),
        *(turned, p_turned, sent, p_sent, h_basis, h_sent, p_sum),
    )
    (total,) = kernel(own_kernel, 0.6, (wide,), near_p, near_h, sent, p_sent, h_sent, energy)
    near, right = kernel(cross_kernel, 0.5, (table, table), turned, sent, l_basis)
    (l_back,) = kernel(light_kernel, 0.2, (narrow,), near, right, rows, l_rows)
    (total,) = kernel(rest_kernel, 0.3, (wide,), near, sent, l_sent, total)
    for piece, route in ((h_back, to_h), (p_back, to_p), (l_back, to_l)):
        total = total + moved(piece, back(route)).astype(F32)
    return total[None, None]


def solution(mesh):
    ni, nj = (mesh.shape[a] for a in AXES)
    assert ni % 2 == 0 and nj % 2 == 0 and min(ni, nj) > 2
    placed = (
        P("iblk", "jblk", None, None, None),
        P("iblk", "jblk", None, None, None),
        P("iblk", "jblk", None, None),
        P(),
        P("iblk", "jblk", None, None, None),
        P("iblk", "jblk", None),
    )

    def body(*arguments):
        return on_device(routes(ni, nj), 2, *arguments)

    return jax.shard_map(
        body,
        mesh=mesh,
        in_specs=placed,
        out_specs=P("iblk", "jblk", None, None, None),
        check_vma=False,
    )
```

```python
import functools

import jax
import jax.numpy as jnp
from jax import lax
from jax.experimental import pallas as pl
from jax.experimental.pallas import tpu as pltpu
from jax.sharding import PartitionSpec as P


F32, BF16, I32 = jnp.float32, jnp.bfloat16, jnp.int32
AXES = ("iblk", "jblk")
PARTS = 3
ROLES = 4
OWN, PARTNER, HEAVY, LIGHT = range(ROLES)
OP, OH, PH, OL = range(4)
META = 16
LANES = 128


def routes(ni, nj):
    def flow(i, j):
        return (1 if j % 2 == 0 else -1), (1 if i % 2 == 1 else -1)

    def along_i(i, j):
        return (i - 2 * flow(i, j)[0]) % ni, j

    def along_j(i, j):
        return i, (j - 2 * flow(i, j)[1]) % nj

    def odd(i, j):
        return (i + j) % 2 == 1

    picks = (
        lambda i, j: (i ^ 1, j) if odd(i, j) else (i, j ^ 1),
        lambda i, j: along_i(i, j) if odd(i, j) else along_j(i, j),
        lambda i, j: along_j(i, j) if odd(i, j) else along_i(i, j),
    )
    made = []
    for pick in picks:
        pairs = []
        for i in range(ni):
            for j in range(nj):
                si, sj = pick(i, j)
                pairs.append((si * nj + sj, i * nj + j))
        made.append(pairs)
    return made


def back(route):
    return [(b, a) for a, b in route]


def dot(a, b):
    return lax.dot_general(a, b, (((1,), (0,)), ((), ())), preferred_element_type=F32)


def dot_nt(a, b):
    return lax.dot_general(a, b, (((1,), (1,)), ((), ())), preferred_element_type=F32)


def two_blocks(a, b):
    zero = jnp.zeros_like(a)
    return jnp.concatenate(
        [jnp.concatenate([a, zero], 1), jnp.concatenate([zero, b], 1)], 0
    )


def prep_kernel(
    reach, plan_hbm, counts_hbm, fock_hbm, amps_hbm, energy_hbm, sent, table_out, energy,
    plan, counts, fock, sems,
):
    pairs, width, _ = amps_hbm.shape
    copies = [
        pltpu.make_async_copy(src, dst, sems.at[k])
        for k, (src, dst) in enumerate(
            [(plan_hbm, plan), (counts_hbm, counts), (fock_hbm, fock), (energy_hbm, energy)]
            + [(amps_hbm.at[p], sent.at[pl.ds(p * width, width)]) for p in range(pairs)]
        )
    ]
    for copy in copies:
        copy.start()
    _, steps, slots = plan.shape
    i, j = lax.axis_index(AXES[0]) % 2, lax.axis_index(AXES[1]) % 2
    forward = (1 - j, i)
    i_heavy = (i + j) % 2
    lane = lax.broadcasted_iota(I32, (META, LANES), 1)
    row = lax.broadcasted_iota(I32, (META, LANES), 0)
    table = jnp.zeros((META, LANES), F32)
    for copy in copies[:3]:
        copy.wait()
    for t in range(steps):
        axis, far = t // reach, t % reach
        heavy = i_heavy if axis == 0 else 1 - i_heavy
        ahead = forward[axis]
        if far:
            role_h, slot_h = jnp.where(ahead == 1, OWN, HEAVY), OH
            role_l, slot_l = jnp.where(ahead == 1, OWN, LIGHT), OL
        else:
            role_h, slot_h = jnp.where(ahead == 1, OWN, HEAVY), jnp.where(ahead == 1, OP, PH)
            role_l, slot_l = PARTNER, jnp.where(ahead == 1, PH, OP)
        role = jnp.where(heavy == 1, role_h, role_l)
        slot = jnp.where(heavy == 1, slot_h, slot_l)
        base = slot * (pairs * pairs)
        live = counts[t]

        def place(c, weight):
            p, q = plan[0, t, c], plan[1, t, c]
            at = base + jnp.where(ahead == 1, p * pairs + q, q * pairs + p)
            value = jnp.where(c < live, fock[plan[2, t, c]], jnp.float32(0.0))
            return jnp.where(lane == at, value, weight)

        weight = lax.fori_loop(0, slots, place, jnp.zeros((META, LANES), F32), unroll=True)
        high = weight.astype(BF16).astype(F32)
        rest = weight - high
        middle = rest.astype(BF16).astype(F32)
        for part, piece in enumerate((high, middle, rest - middle)):
            table = jnp.where(row == part * ROLES + role, piece + table, table)
    sent[pl.ds(pairs * width, META), :] = table.astype(BF16)
    table_out[...] = table.astype(BF16)
    for copy in copies[3:]:
        copy.wait()


def weight_rows(blocks, slot, pairs):
    row = jnp.zeros((1, LANES), F32)
    tables = [(table.astype(F32), role) for table, role in blocks]
    for part in range(PARTS):
        for table, role in tables:
            at = part * ROLES + role
            row = row + table[at : at + 1]
    shape = (pairs * pairs, LANES)
    mine = lax.broadcasted_iota(I32, shape, 1) == (
        slot * pairs * pairs + lax.broadcasted_iota(I32, shape, 0)
    )
    picked = jnp.sum(jnp.where(mine, row, jnp.float32(0.0)), axis=1, keepdims=True)
    wide = jnp.broadcast_to(picked, shape)
    return [[wide[p * pairs + q : p * pairs + q + 1] for q in range(pairs)] for p in range(pairs)]


def cut(a, r, c, width):
    return a[r * width : (r + 1) * width, c * width : (c + 1) * width]


def intersections(turned, basis):
    return jnp.concatenate(
        [
            dot(turned, jnp.concatenate(basis[k : k + 2], 1)).astype(BF16)
            for k in range(0, len(basis), 2)
        ],
        1,
    )


def half(near, amps, width):
    return jnp.concatenate(
        [
            dot(near[:, k * width : (k + 2) * width], two_blocks(amps[k], amps[k + 1])).astype(BF16)
            for k in range(0, len(amps), 2)
        ],
        1,
    )


def row_terms(near, column_amps, weight, width):
    left = half(near, column_amps, width)
    return [
        sum(
            dot_nt(cut(left, p, q, width), cut(near, p, q, width)) * weight[p][q]
            for q in range(len(column_amps))
        )
        for p in range(len(weight))
    ]


def column_sums(near, right, weight, width):
    return [
        sum(
            dot(cut(right, q, p, width), cut(near, p, q, width)) * weight[p][q]
            for p in range(len(weight))
        )
        for q in range(len(weight[0]))
    ]


def column_terms(near, row_amps, weight, width):
    return column_sums(near, half(near.T, row_amps, width), weight, width)


def bases_of(ref):
    return [ref[p] for p in range(ref.shape[0])]


def amps_of(ref, width):
    return [ref[pl.ds(p * width, width), :] for p in range((ref.shape[0] - META) // width)]


def table_of(ref, role):
    return ref[pl.ds(ref.shape[0] - META, META), :], role


def turn_kernel(basis, turned):
    pairs, _, width = basis.shape
    for p in range(pairs):
        turned[pl.ds(p * width, width), :] = basis[p].T


def near_kernel(own_turned, own_sent, p_basis, p_sent, near, p_turned, p_sum):
    pairs, _, width = p_basis.shape
    bases = bases_of(p_basis)
    for p in range(pairs):
        p_turned[pl.ds(p * width, width), :] = bases[p].T
    weight = weight_rows((table_of(own_sent, OWN), table_of(p_sent, PARTNER)), OP, pairs)
    found = intersections(own_turned[...], bases)
    near[...] = found
    for p, y in enumerate(column_terms(found, amps_of(own_sent, width), weight, width)):
        p_sum[p] = y


def heavy_kernel(
    own_turned, p_turned, own_sent, p_sent, h_basis, h_sent, p_sum, near, p_back, h_back
):
    pairs, _, width = h_basis.shape
    tables = (table_of(own_sent, OWN), table_of(p_sent, PARTNER), table_of(h_sent, HEAVY))
    weight = weight_rows(tables, OH, pairs) + weight_rows(tables, PH, pairs)
    turned = jnp.concatenate([own_turned[...], p_turned[...]], 0)
    found = intersections(turned, bases_of(h_basis))
    near[...] = found[: pairs * width]
    y = column_terms(found, amps_of(own_sent, width) + amps_of(p_sent, width), weight, width)
    x = row_terms(found[pairs * width :], amps_of(h_sent, width), weight[pairs:], width)
    for p in range(pairs):
        p_back[p] = (p_sum[p] + x[p]).astype(BF16)
        h_back[p] = y[p].astype(BF16)


def cross_kernel(own_turned, own_sent, l_basis, near, right):
    width = l_basis.shape[2]
    found = intersections(own_turned[...], bases_of(l_basis))
    near[...] = found
    right[...] = half(found.T, amps_of(own_sent, width), width)


def light_kernel(near, right, own_table, l_table, l_back):
    pairs, width, _ = l_back.shape
    weight = weight_rows((table_of(own_table, OWN), table_of(l_table, LIGHT)), OL, pairs)
    for p, y in enumerate(column_sums(near[...], right[...], weight, width)):
        l_back[p] = y.astype(BF16)


def own_kernel(near_p, near_h, own_sent, p_sent, h_sent, energy, total):
    pairs, width, _ = total.shape
    tables = (table_of(own_sent, OWN), table_of(p_sent, PARTNER), table_of(h_sent, HEAVY))
    weight = weight_rows(tables, OP, pairs), weight_rows(tables, OH, pairs)
    x1 = row_terms(near_p[...], amps_of(p_sent, width), weight[0], width)
    x2 = row_terms(near_h[...], amps_of(h_sent, width), weight[1], width)
    for p, amps in enumerate(amps_of(own_sent, width)):
        across = jnp.broadcast_to(energy[pl.ds(p, 1), :], (width, width))
        total[p] = (across.T + across) * amps.astype(F32) + (x1[p] + x2[p])


def rest_kernel(near, own_sent, l_sent, total_in, total):
    pairs, width, _ = total.shape
    weight = weight_rows((table_of(own_sent, OWN), table_of(l_sent, LIGHT)), OL, pairs)
    for p, x in enumerate(row_terms(near[...], amps_of(l_sent, width), weight, width)):
        total[p] = total_in[p] + x


def last_kernel(total, h_in, p_in, l_in, out, held, sems):
    copies = []
    for p in range(total.shape[0]):
        back_here = h_in[p].astype(F32) + p_in[p].astype(F32)
        held[p] = (total[p] + back_here) + l_in[p].astype(F32)
        copies.append(pltpu.make_async_copy(held.at[p], out.at[p], sems.at[p]))
        copies[-1].start()
    for copy in copies:
        copy.wait()


def on_device(all_routes, reach, pno_basis, amplitudes, pno_energy, fock_values, couplings, counts):
    to_p, to_h, to_l = all_routes
    basis, amps, energy = pno_basis[0, 0], amplitudes[0, 0], pno_energy[0, 0]
    plan, live = couplings[0, 0].transpose(1, 0, 2), counts[0, 0]
    pairs, depth, width = basis.shape
    vmem, hbm = pl.BlockSpec(memory_space=pltpu.VMEM), pl.BlockSpec(memory_space=pl.ANY)
    params = pltpu.CompilerParams(vmem_limit_bytes=48 * 1024 * 1024)
    square = (pairs, width, width)
    wide = jax.ShapeDtypeStruct(square, F32)
    narrow = jax.ShapeDtypeStruct(square, BF16)
    flat = jax.ShapeDtypeStruct((pairs * width, depth), BF16)
    table = jax.ShapeDtypeStruct((pairs * width, pairs * width), BF16)

    def moved(block, route):
        return lax.ppermute(block, AXES, route)

    def kernel(body, terms, shapes, *operands):
        flops = 2 * pairs * pairs * (width * width * depth + 4 * width**3)
        return pl.pallas_call(
            body,
            out_shape=shapes,
            in_specs=[vmem] * len(operands),
            out_specs=(vmem,) * len(shapes),
            compiler_params=params,
            cost_estimate=pl.CostEstimate(
                flops=int(terms * flops), bytes_accessed=2 * basis.size, transcendentals=0
            ),
        )(*operands)

    h_basis = moved(basis, to_h)
    p_basis = moved(basis, to_p)
    given = (plan, live, fock_values, amps, energy)
    sent, rows, energy = pl.pallas_call(
        functools.partial(prep_kernel, reach),
        out_shape=(
            jax.ShapeDtypeStruct((pairs * width + META, width), BF16),
            jax.ShapeDtypeStruct((META, LANES), BF16),
            jax.ShapeDtypeStruct(energy.shape, F32),
        ),
        in_specs=[hbm] * len(given),
        out_specs=(vmem,) * 3,
        scratch_shapes=[
            pltpu.SMEM(plan.shape, I32),
            pltpu.SMEM(live.shape, I32),
            pltpu.SMEM(fock_values.shape, F32),
            pltpu.SemaphoreType.DMA((4 + pairs,)),
        ],
        compiler_params=params,
        name="prep",
    )(*(pltpu.with_memory_space_constraint(x, pltpu.HBM) for x in given))
    h_sent, p_sent = moved(sent, to_h), moved(sent, to_p)
    l_rows, l_basis, l_sent = (
        moved(what, to_l) for what in (rows, basis, sent)
    )
    (turned,) = kernel(turn_kernel, 0, (flat,), basis)
    near_p, p_turned, p_sum = kernel(
        near_kernel, 0.7, (table, flat, wide), turned, sent, p_basis, p_sent
    )
    near_h, p_back, h_back = kernel(
        heavy_kernel,
        1.7,
        (table, narrow, narrow),
        *(turned, p_turned, sent, p_sent, h_basis, h_sent, p_sum),
    )
    (total,) = kernel(own_kernel, 0.6, (wide,), near_p, near_h, sent, p_sent, h_sent, energy)
    near, right = kernel(cross_kernel, 0.5, (table, table), turned, sent, l_basis)
    (l_back,) = kernel(light_kernel, 0.2, (narrow,), near, right, rows, l_rows)
    (total,) = kernel(rest_kernel, 0.3, (wide,), near, sent, l_sent, total)
    returned = [
        moved(piece, back(route))
        for piece, route in ((h_back, to_h), (p_back, to_p), (l_back, to_l))
    ]
    total = pl.pallas_call(
        last_kernel,
        out_shape=wide,
        in_specs=[vmem] * 4,
        out_specs=hbm,
        scratch_shapes=[pltpu.VMEM(square, F32), pltpu.SemaphoreType.DMA((pairs,))],
        compiler_params=params,
        name="last",
    )(total, *returned)
    return total[None, None]


def solution(mesh):
    ni, nj = (mesh.shape[a] for a in AXES)
    assert ni % 2 == 0 and nj % 2 == 0 and min(ni, nj) > 2
    placed = (
        P("iblk", "jblk", None, None, None),
        P("iblk", "jblk", None, None, None),
        P("iblk", "jblk", None, None),
        P(),
        P("iblk", "jblk", None, None, None),
        P("iblk", "jblk", None),
    )

    def body(*arguments):
        return on_device(routes(ni, nj), 2, *arguments)

    return jax.shard_map(
        body,
        mesh=mesh,
        in_specs=placed,
        out_specs=P("iblk", "jblk", None, None, None),
        check_vma=False,
    )
```
